256 devices in a mesh: seq: 16 (over y, x), fsdp: 16 (over z, core).
Axes of the slice: x: 4, y: 4, z: 8, core: 2. Of those that a mesh axis runs over, the one named last changes fastest.
Arguments:
- kv_cache: bfloat16 [2, 32, 8192, 1280], P(None, 'fsdp', 'seq'), may hold values from -6 to 6
- keep_flags: int32 [32, 8192], P('fsdp', 'seq'), may hold values from 0 to 1, as said below
- block_weights: float32 [32, 8192], P('fsdp', 'seq'), may hold values from 0.05 to 2
- lengths: int32 [32], P('fsdp'), may hold values from 2048 to 8192, as said below
- token_qkv: bfloat16 [32, 3840], P('fsdp'), may hold values from -10 to 10
- stream: bfloat16 [32, 1280], P('fsdp'), may hold values from -0.59765625 to 0.59765625
- w_out: bfloat16 [1280, 1280], P(None, 'fsdp'), may hold values from -0.15625 to 0.15625
- w_up: bfloat16 [1280, 1280], P(None, 'fsdp'), may hold values from -0.15625 to 0.15625
- w_down: bfloat16 [1280, 1280], P(None, 'fsdp'), may hold values from -0.15625 to 0.15625
- w_qkv: bfloat16 [1280, 3840], P(None, 'fsdp'), may hold values from -0.15625 to 0.15625
- mlp_gain: float32 [1280], replicated, may hold values from 0.1 to 1.9
- next_gain: float32 [1280], replicated, may hold values from 0.1 to 1.9
Outputs:
- packed_cache: bfloat16 [2, 32, 8192, 1280], P(None, 'fsdp', 'seq')
- block_summary: bfloat16 [2, 32, 512, 1280], P(None, 'fsdp', 'seq')
- layer_out: bfloat16 [32, 1280], P('fsdp', 'seq')
- next_qkv: bfloat16 [32, 3840], P('fsdp', 'seq')
The draws below stay inside these ranges and needn't reach their ends.
Inputs may be any that keep to these rules, and one draw needn't show every extreme that they name: `keep_flags`: in every draw one request keeps all 512 positions of one aligned block of 512 positions. `lengths`: in every draw some request has 8192 filled positions.
All inputs are finite; a program needn't handle non-finite values.
Results may differ from the reference program's by a relative error of at most 0.02.
Values may be sent and summed in bfloat16 or wider, within the bound.
A program may use at most 128 MiB of HBM per device.

```python
import math
import jax
import jax.numpy as jnp
from jax import lax

D = 1280
H = 16
HD = 80
FF = 1280
L_DEV = 512
BLK = 16
REQS = 32
L = 8192
NBLK = 512
N_SEQ = 16


def common_plan(key):
    folded = jax.random.fold_in(key, 101)
    key_a, key_b, key_c = jax.random.split(folded, 3)
    chosen_req = jax.random.randint(key_a, (), 0, REQS)
    chosen_block = jax.random.randint(key_b, (), 0, L // L_DEV)
    spots = jax.random.randint(key_c, (REQS,), 0, L // 4 - 1)
    return (chosen_req, chosen_block, spots)


def draw_kv_cache(key, part):
    folded = jax.random.fold_in(key, 202)
    base = jnp.clip(jax.random.normal(folded, (2, REQS, L, D), jnp.float32), -6.0, 6.0)
    return base.astype(jnp.bfloat16)


def draw_keep_flags(key, part):
    chosen_req, chosen_block, spots = common_plan(key)
    folded = jax.random.fold_in(key, 404)
    flags = (jax.random.randint(folded, (REQS, L), 0, 4) > 0).astype(jnp.int32)
    request = jnp.arange(REQS)[:, None]
    position = jnp.arange(L)[None, :]
    full = (request == chosen_req) & (position // L_DEV == chosen_block)
    marked = (position == spots[:, None]) | (position == spots[:, None] + 1)
    return jnp.where(full | marked, 1, flags).astype(jnp.int32)


def draw_lengths(key, part):
    chosen_req, chosen_block, spots = common_plan(key)
    folded = jax.random.fold_in(key, 303)
    drawn = jax.random.randint(folded, (REQS,), L // 4, L + 1)
    return jnp.where(jnp.arange(REQS) == chosen_req, L, drawn).astype(jnp.int32)


def draw_token_qkv(key, part):
    key_q, key_k, key_v = jax.random.split(jax.random.fold_in(key, 505), 3)
    query = jnp.clip(jax.random.normal(key_q, (REQS, D), jnp.float32), -6.0, 6.0)
    noise = jnp.clip(jax.random.normal(key_k, (REQS, D), jnp.float32), -6.0, 6.0)
    values = jnp.clip(jax.random.normal(key_v, (REQS, D), jnp.float32), -6.0, 6.0)
    own_key = 0.5 * query + 0.5 * noise
    return jnp.concatenate([query, own_key, values], axis=1).astype(jnp.bfloat16)


def block_levels(rng, dims, cuts, smallest, high):
    def one(dim, shards_of):
        steps = jax.random.uniform(jax.random.fold_in(jax.random.fold_in(rng, 6), dim), (shards_of,), jnp.float32, smallest / len(cuts), high / len(cuts))
        return jnp.repeat(jnp.exp(steps), dims[dim] // shards_of).reshape((-1,) + (1,) * (len(dims) - dim - 1))

    level = one(*cuts[0])
    for cut in cuts[1:]:
        level = level * one(*cut)
    return level


def scatter_about(stream_key, dims, width, limit, pieces=(), kind=jnp.bfloat16):
    level = block_levels(stream_key, dims, pieces, -0.22, 0.18) if pieces else 1.0
    values = jax.random.normal(stream_key, dims, jnp.float32) * width * level
    return jnp.minimum(jnp.maximum(values, -limit), limit).astype(kind)


def setup_inputs(seed: int = 0) -> dict:
    key_list = jax.random.split(jax.random.key(seed), 13)
    kv_cache = draw_kv_cache(jax.random.fold_in(key_list[12], 71), 0)
    keep_flags = draw_keep_flags(jax.random.fold_in(key_list[12], 71), 0)
    block_weights = jnp.clip(jnp.exp(math.log(2.0) - 3.6888794 * jax.random.uniform(key_list[2], (REQS, L), jnp.float32) ** block_levels(key_list[2], (REQS, L), ((0, 16), (1, 16)), -0.2, 0.2)), 0.05, 2.0)
    lengths = draw_lengths(jax.random.fold_in(key_list[12], 71), 0)
    token_qkv = draw_token_qkv(jax.random.fold_in(key_list[12], 71), 0)
    stream = scatter_about(key_list[5], (REQS, D), 0.1, 0.59765625, ((0, 16),))
    w_out = scatter_about(key_list[6], (D, D), D ** -0.5, 0.15625, ((1, 16),))
    w_up = scatter_about(key_list[7], (D, FF), D ** -0.5, 0.15625, ((1, 16),))
    w_down = scatter_about(key_list[8], (FF, D), FF ** -0.5, 0.15625, ((1, 16),))
    w_qkv = scatter_about(key_list[9], (D, 3 * D), D ** -0.5, 0.15625, ((1, 16),))
    mlp_gain = jnp.clip(1.0 + 0.18 * jax.random.normal(key_list[10], (D,), jnp.float32), 0.1, 1.9)
    next_gain = jnp.clip(1.0 + 0.18 * jax.random.normal(key_list[11], (D,), jnp.float32), 0.1, 1.9)
    return dict(kv_cache=kv_cache, keep_flags=keep_flags, block_weights=block_weights, lengths=lengths, token_qkv=token_qkv, stream=stream, w_out=w_out, w_up=w_up, w_down=w_down, w_qkv=w_qkv, mlp_gain=mlp_gain, next_gain=next_gain)


def normalize(values, gain):
    wide = values.astype(jnp.float32)
    factor = lax.rsqrt(lax.optimization_barrier(jnp.mean(wide * wide, axis=-1, keepdims=True)) + 1e-06)
    return (wide * factor * gain).astype(jnp.bfloat16)

def reference(kv_cache, keep_flags, block_weights, lengths, token_qkv, stream, w_out, w_up, w_down, w_qkv, mlp_gain, next_gain):
    inv_root = 1.0 / math.sqrt(HD)

    def one_request(index, stores):
        packed_all, summary_all, attn_all = stores
        entries = lax.dynamic_index_in_dim(kv_cache, index, 1, keepdims=False)
        flags = lax.dynamic_index_in_dim(keep_flags, index, 0, keepdims=False)
        weights = lax.dynamic_index_in_dim(block_weights, index, 0, keepdims=False)
        length = lax.dynamic_index_in_dim(lengths, index, 0, keepdims=False)
        token = lax.dynamic_index_in_dim(token_qkv, index, 0, keepdims=False)
        position = jnp.arange(L, dtype=jnp.int32)
        in_range = position < length
        kept_rows = in_range & (flags == 1)
        drop_rows = in_range & (flags == 0)
        kept_int = kept_rows.astype(jnp.int32)
        rank = jnp.cumsum(kept_int) - kept_int
        target = rank % N_SEQ * L_DEV + rank // N_SEQ
        target = jnp.where(kept_rows, target, L).astype(jnp.int32)
        packed = jnp.zeros((2, L, D), jnp.bfloat16).at[:, target].set(entries, mode='drop')
        drop_weight = jnp.where(drop_rows, weights, jnp.float32(0.0)).reshape(NBLK, BLK)
        weight_total = lax.optimization_barrier(jnp.sum(drop_weight, axis=1))
        drop_count = lax.optimization_barrier(jnp.sum(drop_rows.reshape(NBLK, BLK).astype(jnp.int32), axis=1))
        sums = jnp.einsum('bk,cbkd->cbd', drop_weight, entries.astype(jnp.float32).reshape(2, NBLK, BLK, D), precision=lax.Precision.HIGHEST)
        summary = (sums / jnp.maximum(weight_total, 1.0)[None, :, None]).astype(jnp.bfloat16)
        query = token[:D].astype(jnp.float32).reshape(H, HD)
        keys = jnp.concatenate([entries[0], summary[0], token[D:2 * D][None]], axis=0).astype(jnp.float32).reshape(-1, H, HD)
        values = jnp.concatenate([entries[1], summary[1], token[2 * D:][None]], axis=0).astype(jnp.float32).reshape(-1, H, HD)
        usable = jnp.concatenate([kept_rows, drop_count > 0, jnp.ones((1,), bool)])
        scores = jnp.einsum('he,nhe->hn', query, keys) * inv_root
        scores = jnp.where(usable[None, :], scores, -jnp.inf)
        peak = lax.optimization_barrier(jnp.max(scores, axis=1, keepdims=True))
        expo = jnp.where(usable[None, :], jnp.exp(scores - peak), 0.0)
        probs = expo / lax.optimization_barrier(jnp.sum(expo, axis=1, keepdims=True))
        attended = jnp.einsum('hn,nhe->he', probs, values).reshape(D).astype(jnp.bfloat16)
        packed_all = lax.dynamic_update_index_in_dim(packed_all, packed, index, 1)
        summary_all = lax.dynamic_update_index_in_dim(summary_all, summary, index, 1)
        attn_all = lax.dynamic_update_index_in_dim(attn_all, attended, index, 0)
        return (packed_all, summary_all, attn_all)
    start_state = (jnp.zeros((2, REQS, L, D), jnp.bfloat16), jnp.zeros((2, REQS, NBLK, D), jnp.bfloat16), jnp.zeros((REQS, D), jnp.bfloat16))
    packed_cache, block_summary, attended = lax.fori_loop(0, REQS, one_request, start_state)
    mid = (stream.astype(jnp.float32) + jnp.dot(attended, w_out, preferred_element_type=jnp.float32)).astype(jnp.bfloat16)
    normed = normalize(mid, mlp_gain)
    hidden = jax.nn.silu(jnp.dot(normed, w_up, preferred_element_type=jnp.float32)).astype(jnp.bfloat16)
    layer_out = (mid.astype(jnp.float32) + jnp.dot(hidden, w_down, preferred_element_type=jnp.float32)).astype(jnp.bfloat16)
    next_qkv = jnp.dot(normalize(layer_out, next_gain), w_qkv, preferred_element_type=jnp.float32).astype(jnp.bfloat16)
    return (packed_cache, block_summary, layer_out, next_qkv)
```

```python
import math

import jax
import jax.numpy as jnp
from jax import lax
from jax.sharding import PartitionSpec as P

H = 16
BLK = 16


neg_fill = -1e30


def normalize(values, gain):
    wide = values.astype(jnp.float32)
    factor = lax.rsqrt(jnp.mean(wide * wide, axis=-1, keepdims=True) + 1e-06)
    return (wide * factor * gain).astype(jnp.bfloat16)


def combine_parts(first, second):
    peak_a, total_a, accum_a = first
    peak_b, total_b, accum_b = second
    peak = jnp.maximum(peak_a, peak_b)
    factor_a = jnp.exp(peak_a - peak)
    factor_b = jnp.exp(peak_b - peak)
    return (
        peak,
        total_a * factor_a + total_b * factor_b,
        accum_a * factor_a[..., None] + accum_b * factor_b[..., None],
    )


def partial_softmax(queries, keys, values, usable, inv_root):
    scores = (
        jnp.einsum("rhe,rnhe->rhn", queries, keys, preferred_element_type=jnp.float32) * inv_root
    )
    scores = jnp.where(usable[:, None, :], scores, neg_fill)
    peak = jnp.max(scores, axis=-1)
    expo = jnp.where(usable[:, None, :], jnp.exp(scores - peak[..., None]), 0.0)
    total = jnp.sum(expo, axis=-1)
    accum = jnp.einsum("rhn,rnhe->rhe", expo, values, preferred_element_type=jnp.float32)
    return (peak, total, accum)


def split_heads(block):
    return block.reshape(block.shape[:-1] + (H, block.shape[-1] // H))


def body(
    kv_cache,
    keep_flags,
    block_weights,
    lengths,
    token_qkv,
    stream,
    w_out,
    w_up,
    w_down,
    w_qkv,
    mlp_gain,
    next_gain,
):
    seq_count = lax.axis_size("seq")
    seq_here = lax.axis_index("seq")
    reqs = kv_cache.shape[1]
    rows = kv_cache.shape[2]
    width = kv_cache.shape[3]
    head_size = width // H
    inv_root = 1.0 / math.sqrt(head_size)
    position = seq_here * rows + jnp.arange(rows, dtype=jnp.int32)
    in_range = position[None, :] < lengths[:, None]
    kept_rows = in_range & (keep_flags == 1)
    drop_rows = in_range & (keep_flags == 0)
    inclusive = jnp.cumsum(kept_rows.astype(jnp.int32), axis=1)
    held = inclusive[:, -1]
    every = lax.all_gather(held, "seq", axis=0)
    source = jnp.arange(seq_count, dtype=jnp.int32)
    lower = source[:, None] < seq_here
    before = jnp.sum(jnp.where(lower, every, 0), axis=0)
    blocks = rows // BLK
    drop_weight = jnp.where(drop_rows, block_weights, 0.0).reshape(reqs, blocks, BLK)
    weight_total = jnp.sum(drop_weight, axis=-1)
    drop_count = jnp.sum(drop_rows.reshape(reqs, blocks, BLK).astype(jnp.int32), axis=-1)
    sums = jnp.einsum(
        "rbk,crbkd->crbd",
        drop_weight,
        kv_cache.reshape(2, reqs, blocks, BLK, width),
        preferred_element_type=jnp.float32,
        precision=lax.Precision.HIGHEST,
    )
    block_summary = (sums / jnp.maximum(weight_total, 1.0)[None, :, :, None]).astype(jnp.bfloat16)
    queries = split_heads(token_qkv[:, :width])
    own_keys = split_heads(token_qkv[:, width : 2 * width])
    own_values = split_heads(token_qkv[:, 2 * width :])

    slot = rows // seq_count
    target = jnp.arange(seq_count, dtype=jnp.int32)
    offset = jnp.mod(target[:, None] - before[None, :], seq_count)
    wanted = offset[:, :, None] + seq_count * jnp.arange(slot, dtype=jnp.int32)[None, None, :]
    local_rank = inclusive - 1
    wanted_r = jnp.transpose(wanted, (1, 0, 2))
    pick_send = (
        kept_rows[:, None, None, :] & (local_rank[:, None, None, :] == wanted_r[:, :, :, None])
    ).astype(jnp.bfloat16)
    outgoing = jnp.einsum(
        "rtsp,crpd->ctrsd", pick_send, kv_cache, preferred_element_type=jnp.float32
    ).astype(jnp.bfloat16)
    incoming = lax.all_to_all(outgoing, "seq", split_axis=1, concat_axis=1, tiled=True)
    before_all = jnp.sum(jnp.where(source[:, None] > source[None, :], 1, 0)[:, :, None]
                         * every[None, :, :], axis=1)
    offset_in = jnp.mod(seq_here - before_all, seq_count)
    counts_in = jnp.maximum((every - offset_in + seq_count - 1) // seq_count, 0)
    ends = jnp.cumsum(counts_in, axis=0)
    starts = ends - counts_in
    local_rows = jnp.arange(rows, dtype=jnp.int32)
    slot_index = jnp.arange(slot, dtype=jnp.int32)
    starts_r = starts.T
    counts_r = counts_in.T
    valid_slot = slot_index[None, None, :] < counts_r[:, :, None]
    dest_row = starts_r[:, :, None] + slot_index[None, None, :]
    pick_recv = (
        valid_slot[:, None, :, :] & (dest_row[:, None, :, :] == local_rows[None, :, None, None])
    ).astype(jnp.bfloat16)
    packed_cache = jnp.einsum(
        "rlts,ctrsd->crld", pick_recv, incoming, preferred_element_type=jnp.float32
    ).astype(jnp.bfloat16)

    row_part = partial_softmax(
        queries, split_heads(kv_cache[0]), split_heads(kv_cache[1]), kept_rows, inv_root
    )
    summary_part = partial_softmax(
        queries,
        split_heads(block_summary[0]),
        split_heads(block_summary[1]),
        drop_count > 0,
        inv_root,
    )
    peak, total, accum = combine_parts(row_part, summary_part)
    packed_parts = jnp.concatenate([peak[..., None], total[..., None], accum], axis=-1)
    gathered = lax.all_gather(packed_parts, "seq", axis=0)
    peak_all = gathered[..., 0]
    top = jnp.max(peak_all, axis=0)
    scale = jnp.exp(peak_all - top[None])
    total = jnp.sum(gathered[..., 1] * scale, axis=0)
    accum = jnp.sum(gathered[..., 2:] * scale[..., None], axis=0)
    peak = top
    own_score = (
        jnp.einsum("rhe,rhe->rh", queries, own_keys, preferred_element_type=jnp.float32) * inv_root
    )
    top_score = jnp.maximum(peak, own_score)
    factor_old = jnp.exp(peak - top_score)
    factor_own = jnp.exp(own_score - top_score)
    attended = (
        accum * factor_old[..., None] + factor_own[..., None] * own_values.astype(jnp.float32)
    ) / (total * factor_old + factor_own)[..., None]
    attended = attended.reshape(reqs, width).astype(jnp.bfloat16)
    fsdp_here = lax.axis_index("fsdp")

    def widen(columns):
        return lax.all_gather(columns, "fsdp", axis=1, tiled=True)

    def own_columns(full, count):
        return lax.dynamic_slice_in_dim(full, fsdp_here * count, count, 1)

    both = lax.all_gather(jnp.concatenate([attended, stream], axis=1), "fsdp", axis=0, tiled=True)
    attn_all = both[:, :width]
    stream_all = both[:, width:]
    mid_cols = own_columns(stream_all, w_out.shape[1]).astype(jnp.float32) + jnp.dot(
        attn_all, w_out, preferred_element_type=jnp.float32
    )
    mid = widen(mid_cols.astype(jnp.bfloat16))
    hidden = widen(
        jax.nn.silu(
            jnp.dot(normalize(mid, mlp_gain), w_up, preferred_element_type=jnp.float32)
        ).astype(jnp.bfloat16)
    )
    out_cols = own_columns(mid, w_down.shape[1]).astype(jnp.float32) + jnp.dot(
        hidden, w_down, preferred_element_type=jnp.float32
    )
    layer_all = widen(out_cols.astype(jnp.bfloat16))
    qkv_all = widen(
        jnp.dot(normalize(layer_all, next_gain), w_qkv, preferred_element_type=jnp.float32).astype(
            jnp.bfloat16
        )
    )
    layer_rows = lax.dynamic_slice_in_dim(layer_all, fsdp_here * reqs, reqs, 0)
    qkv_rows = lax.dynamic_slice_in_dim(qkv_all, fsdp_here * reqs, reqs, 0)
    layer_width = width // seq_count
    qkv_width = 3 * width // seq_count
    layer_out = lax.dynamic_slice_in_dim(layer_rows, seq_here * layer_width, layer_width, 1)
    next_qkv = lax.dynamic_slice_in_dim(qkv_rows, seq_here * qkv_width, qkv_width, 1)
    return (packed_cache, block_summary, layer_out, next_qkv)


def solution(mesh):
    placed = (
        P(None, "fsdp", "seq", None),
        P("fsdp", "seq"),
        P("fsdp", "seq"),
        P("fsdp"),
        P("fsdp", None),
        P("fsdp", None),
        P(None, "fsdp"),
        P(None, "fsdp"),
        P(None, "fsdp"),
        P(None, "fsdp"),
        P(),
        P(),
    )
    return jax.shard_map(
        body,
        mesh=mesh,
        in_specs=placed,
        out_specs=(
            P(None, "fsdp", "seq", None),
            P(None, "fsdp", "seq", None),
            P("fsdp", "seq"),
            P("fsdp", "seq"),
        ),
        check_vma=False,
    )
```
